32 devices in a mesh: dp: 8 (over y, x, core), tensor: 4 (over z).
Axes of the slice: x: 2, y: 2, z: 4, core: 2. Of those that a mesh axis runs over, the one named last changes fastest.
Arguments:
- tokens: bfloat16 [8192, 1024], P('dp'), may hold values from -6 to 6
- cotangent: bfloat16 [8192, 1024], P('dp'), may hold values from -6 to 6
- seq_lengths: int32 [8, 8], P('dp'), may hold values from 0 to 1024, as said below
- norm_gain: float32 [1024], replicated, may hold values from 0.5 to 1.5
- proj_gate: bfloat16 [1024, 2048], P(None, 'tensor'), may hold values from -0.1875 to 0.1875
- proj_value: bfloat16 [1024, 2048], P(None, 'tensor'), may hold values from -0.1875 to 0.1875
- proj_pair: bfloat16 [1024, 256], replicated, may hold values from -0.1875 to 0.1875
- proj_step: bfloat16 [1024, 32], P(None, 'tensor'), may hold values from -0.1875 to 0.1875
- conv_value: float32 [4, 2048], P(None, 'tensor'), may hold values from -3 to 3
- conv_value_bias: float32 [2048], P('tensor'), may hold values from -0.5 to 0.5
- conv_pair: float32 [4, 256], replicated, may hold values from -3 to 3
- conv_pair_bias: float32 [256], replicated, may hold values from -0.5 to 0.5
- step_bias: float32 [32], P('tensor'), may hold values from -4 to -1
- log_rate: float32 [32], P('tensor'), may hold values from 0 to 2.8
- skip_gain: float32 [32], P('tensor'), may hold values from 0.5 to 1.5
- gate_gain: float32 [2048], P('tensor'), may hold values from 0.5 to 1.5
- proj_out: bfloat16 [2048, 1024], P('tensor'), may hold values from -0.125 to 0.125
Outputs:
- block_out: bfloat16 [8192, 1024], P(('dp', 'tensor'))
- grad_tokens: bfloat16 [8192, 1024], P('dp')
- grad_norm_gain: float32 [1024], replicated
- grad_proj_gate: float32 [1024, 2048], P(None, 'tensor')
- grad_proj_value: float32 [1024, 2048], P(None, 'tensor')
- grad_proj_pair: float32 [1024, 256], replicated
- grad_proj_step: float32 [1024, 32], P(None, 'tensor')
- grad_conv_value: float32 [4, 2048], P(None, 'tensor')
- grad_conv_value_bias: float32 [2048], P('tensor')
- grad_conv_pair: float32 [4, 256], replicated
- grad_conv_pair_bias: float32 [256], replicated
- grad_step_bias: float32 [32], P('tensor')
- grad_log_rate: float32 [32], P('tensor')
- grad_skip_gain: float32 [32], P('tensor')
- grad_gate_gain: float32 [2048], P('tensor')
- grad_proj_out: float32 [2048, 1024], P('tensor')
The draws below stay inside these ranges and needn't reach their ends.
Inputs may be any that keep to these rules, and one draw needn't show every extreme that they name: `seq_lengths`: row p lists the lengths of the sequences packed in order from the first of the 1024 rows of pack p; a zero is an unused slot; each row sums to at most 1024, and rows past that sum are padding.
All inputs are finite; a program needn't handle non-finite values.
Results may differ from the reference program's by a relative error of at most 0.0098.
Values sent between devices are 32-bit elements; how exact they have to be, the bound alone decides.
No kernel may reach another device: no remote copies, remote signals or barrier semaphores. Data moves between devices by JAX's collectives and lax.ppermute only.
A program may use at most 128 MiB of HBM per device.

```python
from functools import partial
import jax
import jax.numpy as jnp
from jax import lax

D = 1024
H = 32
STATE = 128
KERNEL = 4
GROUP = 256
DI = 2048
SLOTS = 8
TOK_DEV = 1024
TOKENS = 8192
N_DP = 8


def draw_seq_lengths(key, part):
    base_key = jax.random.fold_in(key, 11)
    key_total, key_full, key_cuts = jax.random.split(base_key, 3)
    totals = jax.random.randint(key_total, (N_DP,), TOK_DEV // 4, TOK_DEV + 1, dtype=jnp.int32)
    full_row = jax.random.randint(key_full, (), 0, N_DP, dtype=jnp.int32)
    cut_points = jnp.sort(jax.random.randint(key_cuts, (N_DP, SLOTS - 1), 0, TOK_DEV + 1, dtype=jnp.int32), axis=1)
    cut_points = cut_points * totals[:, None] // TOK_DEV
    edge_list = jnp.concatenate([jnp.zeros((N_DP, 1), jnp.int32), cut_points, totals[:, None]], axis=1)
    spread = edge_list[:, 1:] - edge_list[:, :-1]
    single = jnp.concatenate([jnp.full((1,), TOK_DEV, jnp.int32), jnp.zeros((SLOTS - 1,), jnp.int32)])
    row_ids = jnp.arange(N_DP, dtype=jnp.int32)
    return jnp.where((row_ids == full_row)[:, None], single[None, :], spread).astype(jnp.int32)


def level_of(stream_key, shape, shards, smallest, largest):
    gain, own = 1.0, jax.random.fold_in(stream_key, 6)
    for dim, parts in shards:
        heights = jnp.exp(jax.random.uniform(jax.random.fold_in(own, dim), (parts,), jnp.float32, smallest / len(shards), largest / len(shards)))
        gain = gain * jnp.repeat(heights, shape[dim] // parts).reshape([-1 if axis == dim else 1 for axis in range(len(shape))])
    return gain


def scatter_about(rng, shape, scale, most, cuts=(), kind=jnp.bfloat16):
    factor_of = level_of(rng, shape, cuts, -0.22, 0.18) if cuts else 1.0
    entries = jax.random.normal(rng, shape, jnp.float32) * scale * factor_of
    return jnp.minimum(jnp.maximum(entries, -most), most).astype(kind)


def setup_inputs(seed: int = 0) -> dict:
    splits = jax.random.split(jax.random.key(seed), 18)
    tokens = scatter_about(splits[0], (TOKENS, D), 1.0, 6.0, ((0, 8),))
    cotangent = scatter_about(splits[1], (TOKENS, D), 1.0, 6.0, ((0, 8),))
    seq_lengths = draw_seq_lengths(jax.random.fold_in(splits[17], 71), 0)
    norm_gain = jnp.clip(1.0 + 0.1 * jax.random.normal(splits[3], (D,), jnp.float32), 0.5, 1.5)
    proj_gate = scatter_about(splits[4], (D, DI), D ** -0.5, 0.1875, ((1, 4),))
    proj_value = scatter_about(splits[5], (D, DI), D ** -0.5, 0.1875, ((1, 4),))
    proj_pair = scatter_about(splits[6], (D, 2 * STATE), D ** -0.5, 0.1875)
    proj_step = scatter_about(splits[7], (D, H), D ** -0.5, 0.1875, ((1, 4),))
    conv_value = scatter_about(splits[8], (KERNEL, DI), KERNEL ** -0.5, 3.0, ((1, 4),), jnp.float32)
    conv_value_bias = jnp.clip(jax.random.uniform(splits[9], (DI,), jnp.float32, -0.5, 0.5) * level_of(splits[9], (DI,), ((0, 4),), -0.4, 0.0), -0.5, 0.5)
    conv_pair = scatter_about(splits[10], (KERNEL, 2 * STATE), KERNEL ** -0.5, 3.0, (), jnp.float32)
    conv_pair_bias = jnp.clip(jax.random.uniform(splits[11], (2 * STATE,), jnp.float32, -0.5, 0.5), -0.5, 0.5)
    step_bias = jnp.clip(-4.0 + 3.0 * jax.random.uniform(splits[12], (H,), jnp.float32) ** level_of(splits[12], (H,), ((0, 4),), -0.2, 0.2), -4.0, -1.0)
    log_rate = jnp.clip(2.8 * jax.random.uniform(splits[13], (H,), jnp.float32) ** level_of(splits[13], (H,), ((0, 4),), -0.2, 0.2), 0.0, 2.8)
    skip_gain = jnp.clip(0.5 + 1.0 * jax.random.uniform(splits[14], (H,), jnp.float32) ** level_of(splits[14], (H,), ((0, 4),), -0.2, 0.2), 0.5, 1.5)
    gate_gain = jnp.clip(1.0 + 0.1 * jax.random.normal(splits[15], (DI,), jnp.float32), 0.5, 1.5)
    proj_out = scatter_about(splits[16], (DI, D), DI ** -0.5, 0.125, ((0, 4),))
    return dict(tokens=tokens, cotangent=cotangent, seq_lengths=seq_lengths, norm_gain=norm_gain, proj_gate=proj_gate, proj_value=proj_value, proj_pair=proj_pair, proj_step=proj_step, conv_value=conv_value, conv_value_bias=conv_value_bias, conv_pair=conv_pair, conv_pair_bias=conv_pair_bias, step_bias=step_bias, log_rate=log_rate, skip_gain=skip_gain, gate_gain=gate_gain, proj_out=proj_out)


epsilon = 1e-05
HIGHEST = lax.Precision.HIGHEST

def segment_ids(lengths_row, row_count):
    bounds = jnp.cumsum(lengths_row).astype(jnp.int32)
    position = jnp.arange(row_count, dtype=jnp.int32)
    segment = lax.optimization_barrier(jnp.sum((position[:, None] >= bounds[None, :]).astype(jnp.int32), axis=1)).astype(jnp.int32)
    live_mask = (position < bounds[-1]).astype(jnp.float32)
    return (segment, live_mask)

def conv_silu(pre_act, weight, conv_bias, segment):
    row_count = pre_act.shape[0]
    tap_count = weight.shape[0]
    summed = conv_bias[None, :] + weight[tap_count - 1][None, :] * pre_act
    for offset in range(1, tap_count):
        shifted = jnp.pad(pre_act, ((offset, 0), (0, 0)))[:row_count]
        shifted_seg = jnp.pad(segment, (offset, 0), constant_values=-1)[:row_count]
        same_seq = (shifted_seg == segment).astype(jnp.float32)
        summed = summed + weight[tap_count - 1 - offset][None, :] * shifted * same_seq[:, None]
    return jax.nn.silu(summed)

def ssd_gate(gate_pre, value_post, pair_post, step_pre, step_bias, log_rate, skip_gain, segment):
    row_count = value_post.shape[0]
    head_count = step_pre.shape[1]
    head_dim = value_post.shape[1] // head_count
    state_dim = pair_post.shape[1] // 2
    block_count = row_count // GROUP
    step_size = jax.nn.softplus(step_pre + step_bias[None, :])
    rate_per = -jnp.exp(log_rate)
    log_decay = step_size * rate_per[None, :]
    values = value_post.reshape(row_count, head_count, head_dim)
    scaled = (values * step_size[:, :, None]).reshape(block_count, GROUP, head_count, head_dim)
    cumulative = jnp.cumsum(log_decay.reshape(block_count, GROUP, head_count), axis=1)
    seg_blocks = segment.reshape(block_count, GROUP)
    b_blocks = pair_post[:, :state_dim].reshape(block_count, GROUP, state_dim)
    c_blocks = pair_post[:, state_dim:].reshape(block_count, GROUP, state_dim)
    lower_tri = jnp.arange(GROUP)[:, None] >= jnp.arange(GROUP)[None, :]
    same_seq = (seg_blocks[:, :, None] == seg_blocks[:, None, :]) & lower_tri[None]
    log_gap = cumulative[:, :, None, :] - cumulative[:, None, :, :]
    decay_mat = jnp.where(same_seq[..., None], jnp.exp(jnp.where(same_seq[..., None], log_gap, 0.0)), 0.0)
    scores = jnp.einsum('cin,cjn->cij', c_blocks, b_blocks, precision=HIGHEST)
    weights = scores[..., None] * decay_mat
    intra_out = jnp.einsum('cijh,cjhp->cihp', weights, scaled, precision=HIGHEST)
    before = jnp.concatenate([jnp.full((1,), -1, jnp.int32), seg_blocks[:-1, -1].astype(jnp.int32)])
    end_same = (seg_blocks == seg_blocks[:, -1:]).astype(jnp.float32)
    to_end = jnp.exp(cumulative[:, -1:, :] - cumulative) * end_same[:, :, None]
    local_states = jnp.einsum('cjh,cjn,cjhp->chnp', to_end, b_blocks, scaled, precision=HIGHEST)
    carry_in = jnp.exp(cumulative) * (seg_blocks == before[:, None]).astype(jnp.float32)[:, :, None]
    passes = jnp.exp(cumulative[:, -1, :]) * (seg_blocks[:, -1] == before).astype(jnp.float32)[:, None]

    def advance(state_now, inputs):
        c_block, carry_row, local_state, pass_row = inputs
        inter_out = jnp.einsum('in,hnp->ihp', c_block, state_now, precision=HIGHEST) * carry_row[:, :, None]
        return (local_state + pass_row[:, None, None] * state_now, inter_out)
    start_state = jnp.zeros((head_count, state_dim, head_dim), jnp.float32)
    final_state, inter_all = lax.scan(advance, start_state, (c_blocks, carry_in, local_states, passes))
    mixed_out = (intra_out + inter_all).reshape(row_count, head_count * head_dim)
    mixed_out = mixed_out + jnp.repeat(skip_gain, head_dim)[None, :] * value_post
    return mixed_out * jax.nn.silu(gate_pre)

def mixer_rest(gate_pre, value_pre, pair_post, step_pre, conv_value, conv_value_bias, step_bias, log_rate, skip_gain, segment):
    value_post = conv_silu(value_pre, conv_value, conv_value_bias, segment)
    return ssd_gate(gate_pre, value_post, pair_post, step_pre, step_bias, log_rate, skip_gain, segment)

def one_pack(tok_row, cot_row, lengths_row, norm_gain, proj_gate, proj_value, proj_pair, proj_step, conv_value, conv_value_bias, conv_pair, conv_pair_bias, step_bias, log_rate, skip_gain, gate_gain, proj_out):
    row_count = tok_row.shape[0]
    segment, live_mask = segment_ids(lengths_row, row_count)
    widened = tok_row.astype(jnp.float32)
    scale_in = lax.rsqrt(lax.optimization_barrier(jnp.mean(widened * widened, axis=1, keepdims=True)) + epsilon)
    normed = (widened * scale_in * norm_gain[None, :]).astype(jnp.bfloat16)
    gate_pre = jnp.dot(normed, proj_gate, preferred_element_type=jnp.float32)
    value_pre = jnp.dot(normed, proj_value, preferred_element_type=jnp.float32)
    pair_pre = jnp.dot(normed, proj_pair, preferred_element_type=jnp.float32)
    step_pre = jnp.dot(normed, proj_step, preferred_element_type=jnp.float32)
    pair_fn = partial(conv_silu, segment=segment)
    pair_post, pair_back = jax.vjp(pair_fn, pair_pre, conv_pair, conv_pair_bias)
    rest_fn = partial(mixer_rest, segment=segment)
    gated_value, rest_back = jax.vjp(rest_fn, gate_pre, value_pre, pair_post, step_pre, conv_value, conv_value_bias, step_bias, log_rate, skip_gain)
    square_sum = lax.optimization_barrier(jnp.sum(gated_value * gated_value, axis=1, keepdims=True))
    scale_gate = lax.rsqrt(square_sum / DI + epsilon)
    gate_out = (gated_value * scale_gate * gate_gain[None, :]).astype(jnp.bfloat16)
    mixed_out = jnp.dot(gate_out, proj_out, preferred_element_type=jnp.float32)
    out_row = (widened + mixed_out * live_mask[:, None]).astype(jnp.bfloat16)
    cot_live = jnp.where(live_mask[:, None] > 0, cot_row, jnp.zeros_like(cot_row))
    grad_proj_out = jnp.dot(gate_out.T, cot_live, preferred_element_type=jnp.float32)
    grad_gate_out = jnp.dot(cot_live, proj_out.T, preferred_element_type=jnp.float32)
    grad_gate_gain = lax.optimization_barrier(jnp.sum(grad_gate_out * gated_value * scale_gate, axis=0))
    weighted = grad_gate_out * gate_gain[None, :]
    stat_dot = lax.optimization_barrier(jnp.sum(weighted * gated_value, axis=1, keepdims=True))
    grad_gated = weighted * scale_gate - gated_value * (scale_gate ** 3 / DI) * stat_dot
    grads_rest = rest_back(grad_gated)
    grad_pair_pre, grad_conv_pair, grad_conv_pair_bias = pair_back(grads_rest[2])
    low_gate = grads_rest[0].astype(jnp.bfloat16)
    low_value = grads_rest[1].astype(jnp.bfloat16)
    low_step = grads_rest[3].astype(jnp.bfloat16)
    low_pair = grad_pair_pre.astype(jnp.bfloat16)
    grad_proj_gate = jnp.dot(normed.T, low_gate, preferred_element_type=jnp.float32)
    grad_proj_value = jnp.dot(normed.T, low_value, preferred_element_type=jnp.float32)
    grad_proj_pair = jnp.dot(normed.T, low_pair, preferred_element_type=jnp.float32)
    grad_proj_step = jnp.dot(normed.T, low_step, preferred_element_type=jnp.float32)
    grad_normed = jnp.dot(low_gate, proj_gate.T, preferred_element_type=jnp.float32)
    grad_normed = grad_normed + jnp.dot(low_value, proj_value.T, preferred_element_type=jnp.float32)
    grad_normed = grad_normed + jnp.dot(low_step, proj_step.T, preferred_element_type=jnp.float32)
    grad_normed = grad_normed + jnp.dot(low_pair, proj_pair.T, preferred_element_type=jnp.float32)
    grad_norm_gain = lax.optimization_barrier(jnp.sum(grad_normed * widened * scale_in, axis=0))
    scaled_grad = grad_normed * norm_gain[None, :]
    row_dot = lax.optimization_barrier(jnp.sum(scaled_grad * widened, axis=1, keepdims=True))
    grad_wide = scaled_grad * scale_in - widened * (scale_in ** 3 / D) * row_dot
    grad_row = (cot_row.astype(jnp.float32) + grad_wide).astype(jnp.bfloat16)
    grads = (grad_norm_gain, grad_proj_gate, grad_proj_value, grad_proj_pair, grad_proj_step, grads_rest[4], grads_rest[5], grad_conv_pair, grad_conv_pair_bias, grads_rest[6], grads_rest[7], grads_rest[8], grad_gate_gain, grad_proj_out)
    return (out_row, grad_row, grads)

def reference(tokens, cotangent, seq_lengths, norm_gain, proj_gate, proj_value, proj_pair, proj_step, conv_value, conv_value_bias, conv_pair, conv_pair_bias, step_bias, log_rate, skip_gain, gate_gain, proj_out):
    pack_count = seq_lengths.shape[0]
    tok_packs = tokens.reshape(pack_count, -1, D)
    cot_packs = cotangent.reshape(pack_count, -1, D)
    shapes = (norm_gain, proj_gate, proj_value, proj_pair, proj_step, conv_value, conv_value_bias, conv_pair, conv_pair_bias, step_bias, log_rate, skip_gain, gate_gain, proj_out)
    start_grads = tuple((jnp.zeros(item.shape, jnp.float32) for item in shapes))

    def step_fn(grads, inputs):
        tok_row, cot_row, lengths_row = inputs
        out_row, grad_row, new_grads = one_pack(tok_row, cot_row, lengths_row, norm_gain, proj_gate, proj_value, proj_pair, proj_step, conv_value, conv_value_bias, conv_pair, conv_pair_bias, step_bias, log_rate, skip_gain, gate_gain, proj_out)
        return (jax.tree.map(jnp.add, grads, new_grads), (out_row, grad_row))
    grads, outputs = lax.scan(step_fn, start_grads, (tok_packs, cot_packs, seq_lengths))
    block_out = outputs[0].reshape(-1, D)
    grad_tokens = outputs[1].reshape(-1, D)
    return (block_out, grad_tokens, grads[0], grads[1], grads[2], grads[3], grads[4], grads[5], grads[6], grads[7], grads[8], grads[9], grads[10], grads[11], grads[12], grads[13])
```

```python
from functools import partial

import jax
import jax.numpy as jnp
from jax import lax
from jax.experimental import pallas as pl
from jax.experimental.pallas import tpu as pltpu
from jax.sharding import PartitionSpec as P

EPS = 1e-05
HEAD = 64
NEG = -1e30
HI = lax.Precision.HIGHEST
F32 = jnp.float32
BF16 = jnp.bfloat16
NT = (((1,), (1,)), ((), ()))
TN = (((0,), (0,)), ((), ()))


def dot(a, b, dims=(((1,), (0,)), ((), ())), exact=False):
    return lax.dot_general(
        a, b, dims, precision=HI if exact else None, preferred_element_type=F32
    )


def iota(shape, axis):
    return lax.broadcasted_iota(jnp.int32, shape, axis)


def bounds_of(lens_ref, slots):
    ends, total = [], 0
    for s in range(slots):
        total = total + lens_ref[0, s]
        ends.append(total)
    return ends


def segment_of(position, ends):
    seg = jnp.zeros(position.shape, jnp.int32)
    for end in ends:
        seg = seg + (position >= end).astype(jnp.int32)
    return seg


def segment_at(position, ends):
    seg = jnp.int32(0)
    for end in ends:
        seg = seg + (position >= end).astype(jnp.int32)
    return seg


def sigmoid(v):
    return 1.0 / (1.0 + jnp.exp(-v))


def softplus(v):
    return jnp.maximum(v, 0.0) + jnp.log1p(jnp.exp(-jnp.abs(v)))


def spread(cols, heads):
    rows = cols.shape[0]
    low = iota((rows, 2 * HEAD), 1) < HEAD
    parts = []
    for h in range(0, heads, 2):
        a = jnp.broadcast_to(cols[:, h : h + 1], (rows, 2 * HEAD))
        b = jnp.broadcast_to(cols[:, h + 1 : h + 2], (rows, 2 * HEAD))
        parts.append(jnp.where(low, a, b))
    return jnp.concatenate(parts, axis=1)


def conv_pre(buf, block, rows, taps_ref, bias_ref, masks):
    count = taps_ref.shape[0]
    z = bias_ref[...] + taps_ref[count - 1 : count, :] * block
    for k in range(1, count):
        z = z + taps_ref[count - 1 - k : count - k, :] * (
            buf[pl.ds(8 - k, rows), :] * masks[k]
        )
    return z


def scan_terms(step_pre, step_bias, log_rate, ends, base, rows, heads):
    step_size = softplus(step_pre + step_bias)
    rate = -jnp.exp(log_rate)
    decay = step_size * rate
    tril = (iota((rows, rows), 0) >= iota((rows, rows), 1)).astype(F32)
    cum_col = dot(tril, decay, exact=True)
    cum_row = jnp.transpose(cum_col)
    col = segment_of(base + iota((rows, 1), 0), ends)
    row = segment_of(base + iota((1, rows), 1), ends)
    seg_last = segment_at(base + rows - 1, ends)
    seg_before = jnp.where(base > 0, segment_at(base - 1, ends), -1)
    cum_end = cum_col[rows - 1 : rows, :]
    carry_in = jnp.exp(cum_col) * (col == seg_before).astype(F32)
    to_end = jnp.exp(cum_end - cum_col) * (col == seg_last).astype(F32)
    passes = jnp.exp(cum_end) * (seg_last == seg_before).astype(F32)
    return step_size, rate, cum_col, cum_row, col, row, carry_in, to_end, passes


def conv_masks(base, rows, taps, ends, col):
    position = base + iota((rows, 1), 0)
    masks = [None]
    for k in range(1, taps):
        before = segment_of(position - k, ends)
        masks.append(((before == col) & (position >= k)).astype(F32))
    return masks


def forward_kernel(
    lens_ref, tok_ref, cot_ref, gain_ref, wg_ref, wv_ref, wp_ref, ws_ref,
    cv_ref, cvb_ref, cp_ref, cpb_ref, sb_ref, lr_ref, sg_ref, gg_ref, wo_ref,
    normed_ref, gate_ref, value_ref, pair_ref, step_ref, ssd_ref, ggo_ref,
    states_ref, mixed_ref, stats_ref,
    vbuf, pbuf, state,
):
    b = pl.program_id(0)
    rows = tok_ref.shape[0]
    heads = ws_ref.shape[1]
    n = pair_ref.shape[1] // 2
    base = b * rows

    @pl.when(b == 0)
    def _():
        vbuf[0:8, :] = jnp.zeros((8, vbuf.shape[1]), F32)
        pbuf[0:8, :] = jnp.zeros((8, pbuf.shape[1]), F32)
        state[...] = jnp.zeros_like(state)

    ends = bounds_of(lens_ref, lens_ref.shape[1])
    tok = tok_ref[...].astype(F32)
    scale_in = lax.rsqrt(jnp.mean(tok * tok, axis=1, keepdims=True) + EPS)
    normed = (tok * scale_in * gain_ref[...]).astype(BF16)
    normed_ref[...] = normed
    gate_pre = dot(normed, wg_ref[...])
    gate_ref[...] = gate_pre
    value_pre = dot(normed, wv_ref[...])
    value_ref[...] = value_pre
    pair_pre = dot(normed, wp_ref[...])
    pair_ref[...] = pair_pre
    step_pre = dot(normed, ws_ref[...])
    step_ref[...] = step_pre
    vbuf[8:, :] = value_pre
    pbuf[8:, :] = pair_pre

    step_size, rate, cum_col, cum_row, col, row, carry_in, to_end, passes = scan_terms(
        step_pre, sb_ref[...], lr_ref[...], ends, base, rows, heads
    )
    masks = conv_masks(base, rows, cv_ref.shape[0], ends, col)
    zv = conv_pre(vbuf, value_pre, rows, cv_ref, cvb_ref, masks)
    value = zv * sigmoid(zv)
    zp = conv_pre(pbuf, pair_pre, rows, cp_ref, cpb_ref, masks)
    pair = zp * sigmoid(zp)
    vbuf[0:8, :] = vbuf[rows : rows + 8, :]
    pbuf[0:8, :] = pbuf[rows : rows + 8, :]
    b_rows, c_rows = pair[:, :n], pair[:, n:]

    scaled = value * spread(step_size, heads)
    low_scaled = scaled.astype(BF16)
    scores = dot(c_rows, b_rows, NT, exact=True)
    causal = iota((rows, rows), 0) >= iota((rows, rows), 1)
    bar = jnp.where(causal & (col == row), 0.0, NEG)
    low = iota((rows, 2 * HEAD), 1) < HEAD
    parts = []
    for h in range(0, heads, 2):
        lanes = low_scaled[:, h * HEAD : (h + 2) * HEAD]
        outs = []
        for g in (h, h + 1):
            gap = cum_col[:, g : g + 1] - cum_row[g : g + 1, :]
            weights = (scores * jnp.exp(gap + bar)).astype(BF16)
            outs.append(dot(weights, lanes))
        parts.append(jnp.where(low, outs[0], outs[1]))
    prev = state[...]
    states_ref[0] = prev
    ssd = jnp.concatenate(parts, axis=1) + spread(carry_in, heads) * dot(
        c_rows, prev, exact=True
    )
    state[...] = spread(passes, heads) * prev + dot(
        b_rows, low_scaled.astype(F32) * spread(to_end, heads), TN, exact=True
    )
    ssd = ssd + spread(sg_ref[...], heads) * value
    ssd_ref[...] = ssd

    gated = ssd * (gate_pre * sigmoid(gate_pre))
    weighed = gated * gg_ref[...]
    mixed_ref[...] = dot(weighed.astype(BF16), wo_ref[...])
    live = base + iota((rows, 1), 0) < ends[-1]
    cot = jnp.where(live, cot_ref[...].astype(F32), 0.0).astype(BF16)
    ggo = dot(cot, wo_ref[...], NT)
    ggo_ref[...] = ggo
    ones = jnp.ones((8, gated.shape[1]), F32)
    square = dot(ones, gated * gated, NT, exact=True)
    stat = dot(ones, ggo * weighed, NT, exact=True)
    stats_ref[...] = jnp.concatenate([square[0:1, :], stat[0:1, :]], axis=0)


def backward_kernel(
    lens_ref, stats_ref, gate_ref, value_ref, vprev_ref, pair_ref, pprev_ref,
    step_ref, ssd_ref, ggo_ref, states_ref,
    wg_ref, wv_ref, wp_ref, ws_ref,
    cv_ref, cvb_ref, cp_ref, cpb_ref, sb_ref, lr_ref, sg_ref, gg_ref,
    gate_out_ref, lowg_ref, lowv_ref, lowp_ref, lows_ref, grad_ref, scale_ref,
    ggg_ref, gcv_ref, gcvb_ref, gcp_ref, gcpb_ref, gsb_ref, glr_ref, gsg_ref,
    vbuf, pbuf, dvbuf, dpbuf, dstate, dcarry,
    *, channels,
):
    i = pl.program_id(0)
    blocks = pl.num_programs(0)
    b = blocks - 1 - i
    rows = gate_ref.shape[0]
    heads = ws_ref.shape[1]
    n = pair_ref.shape[1] // 2
    taps = cv_ref.shape[0]
    base = b * rows

    @pl.when(i == 0)
    def _():
        dvbuf[rows:, :] = jnp.zeros((8, dvbuf.shape[1]), F32)
        dpbuf[rows:, :] = jnp.zeros((8, dpbuf.shape[1]), F32)
        dstate[...] = jnp.zeros_like(dstate)
        dcarry[...] = jnp.zeros_like(dcarry)
        for ref in (ggg_ref, gcv_ref, gcvb_ref, gcp_ref, gcpb_ref, gsb_ref, glr_ref, gsg_ref):
            ref[...] = jnp.zeros_like(ref)

    ends = bounds_of(lens_ref, lens_ref.shape[1])
    eye = (iota((rows, rows), 0) == iota((rows, rows), 1)).astype(F32)
    stats = dot(eye, stats_ref[...], NT, exact=True)
    scale = lax.rsqrt(stats[:, 0:1] / channels + EPS)
    scale_ref[...] = scale
    pull = scale * scale * scale / channels * stats[:, 1:2]

    gate_pre = gate_ref[...]
    sig_gate = sigmoid(gate_pre)
    silu_gate = gate_pre * sig_gate
    ssd = ssd_ref[...]
    ggo = ggo_ref[...]
    gated = ssd * silu_gate
    scaled_gated = gated * scale
    gate_out_ref[...] = (scaled_gated * gg_ref[...]).astype(BF16)
    ggg_ref[...] += jnp.sum(ggo * scaled_gated, axis=0, keepdims=True)
    grad_gated = ggo * gg_ref[...] * scale - gated * pull
    low_gate = (grad_gated * ssd * (sig_gate * (1.0 + gate_pre * (1.0 - sig_gate)))).astype(BF16)
    lowg_ref[...] = low_gate
    grad_ssd = grad_gated * silu_gate

    step_pre = step_ref[...]
    step_size, rate, cum_col, cum_row, col, row, carry_in, to_end, passes = scan_terms(
        step_pre, sb_ref[...], lr_ref[...], ends, base, rows, heads
    )
    masks = conv_masks(base, rows, taps, ends, col)
    value_pre, pair_pre = value_ref[...], pair_ref[...]
    vbuf[0:8, :] = vprev_ref[...]
    pbuf[0:8, :] = pprev_ref[...]
    vbuf[8:, :] = value_pre
    pbuf[8:, :] = pair_pre
    zv = conv_pre(vbuf, value_pre, rows, cv_ref, cvb_ref, masks)
    sig_v = sigmoid(zv)
    value = zv * sig_v
    zp = conv_pre(pbuf, pair_pre, rows, cp_ref, cpb_ref, masks)
    sig_p = sigmoid(zp)
    pair = zp * sig_p
    b_rows, c_rows = pair[:, :n], pair[:, n:]

    step_wide = spread(step_size, heads)
    scaled = value * step_wide
    low_scaled = scaled.astype(BF16)
    low_grad = grad_ssd.astype(BF16)
    round_scaled = low_scaled.astype(F32)
    round_grad = low_grad.astype(F32)
    skip = spread(sg_ref[...], heads)
    gsg_ref[...] += jnp.sum(grad_ssd * value, axis=0, keepdims=True)

    scores_t = dot(b_rows, c_rows, NT, exact=True)
    causal_t = iota((rows, rows), 0) <= iota((rows, rows), 1)
    bar_t = jnp.where(causal_t & (col == row), 0.0, NEG)
    low = iota((rows, 2 * HEAD), 1) < HEAD
    zero = jnp.zeros((rows, 2 * HEAD), BF16)
    grad_scores_t = jnp.zeros((rows, rows), F32)
    parts = []
    for h in range(0, heads, 2):
        own = slice(h * HEAD, (h + 2) * HEAD)
        lanes_x, lanes_y = low_scaled[:, own], low_grad[:, own]
        outs = []
        for g in (h, h + 1):
            gap = cum_row[g : g + 1, :] - cum_col[:, g : g + 1]
            fall = jnp.exp(gap + bar_t)
            weights = (scores_t * fall).astype(BF16)
            outs.append(dot(weights, lanes_y))
            half = jnp.where(low, lanes_x, zero) if g == h else jnp.where(low, zero, lanes_x)
            grad_scores_t += dot(half, lanes_y, NT) * fall
        parts.append(jnp.where(low, outs[0], outs[1]))
    prev, later = states_ref[0], dstate[...]
    end_wide = spread(to_end, heads)
    carry_grad = round_grad * spread(carry_in, heads)
    grad_scaled = jnp.concatenate(parts, axis=1) + end_wide * dot(b_rows, later, exact=True)
    grad_c = dot(grad_scores_t, b_rows, TN, exact=True) + dot(carry_grad, prev, NT, exact=True)
    grad_b = dot(grad_scores_t, c_rows, exact=True) + dot(
        round_scaled * end_wide, later, NT, exact=True
    )
    dstate[...] = spread(passes, heads) * later + dot(c_rows, carry_grad, TN, exact=True)

    heads_of = (iota((scaled.shape[1], heads), 0) // HEAD == iota((scaled.shape[1], heads), 1)).astype(F32)
    inner = ssd - skip * value
    grad_cum = dot(round_grad * inner - round_scaled * grad_scaled, heads_of, exact=True)
    grad_step = dot(value * grad_scaled, heads_of, exact=True)
    seg_last = segment_at(base + rows - 1, ends)
    seg_after = segment_at(base + rows, ends)
    suffix = (causal_t & (col == row)).astype(F32)
    grad_decay = dot(suffix, grad_cum, exact=True) + dcarry[...] * (
        (col == seg_last) & (seg_last == seg_after)
    ).astype(F32)
    dcarry[...] = grad_decay[0:1, :]
    grad_step = grad_step + grad_decay * rate
    glr_ref[...] += rate * jnp.sum(grad_decay * step_size, axis=0, keepdims=True)
    grad_step_pre = grad_step * sigmoid(step_pre + sb_ref[...])
    gsb_ref[...] += jnp.sum(grad_step_pre, axis=0, keepdims=True)
    low_step = grad_step_pre.astype(BF16)
    lows_ref[...] = low_step

    position = base + iota((rows, 1), 0)
    total = blocks * rows
    after = [None]
    for k in range(1, taps):
        after.append(((segment_of(position + k, ends) == col) & (position + k < total)).astype(F32))

    def conv_back(grad_post, z, sig, block, buf, dbuf, taps_ref, gtaps_ref, gbias_ref):
        dz = grad_post * (sig * (1.0 + z * (1.0 - sig)))
        dbuf[0:rows, :] = dz
        gbias_ref[...] += jnp.sum(dz, axis=0, keepdims=True)
        gtaps_ref[taps - 1 : taps, :] += jnp.sum(dz * block, axis=0, keepdims=True)
        pre = taps_ref[taps - 1 : taps, :] * dz
        for k in range(1, taps):
            gtaps_ref[taps - 1 - k : taps - k, :] += jnp.sum(
                dz * (buf[pl.ds(8 - k, rows), :] * masks[k]), axis=0, keepdims=True
            )
            pre = pre + taps_ref[taps - 1 - k : taps - k, :] * (
                dbuf[pl.ds(k, rows), :] * after[k]
            )
        dbuf[rows:, :] = dz[0:8, :]
        return pre

    grad_value = skip * grad_ssd + step_wide * grad_scaled
    low_value = conv_back(
        grad_value, zv, sig_v, value_pre, vbuf, dvbuf, cv_ref, gcv_ref, gcvb_ref
    ).astype(BF16)
    lowv_ref[...] = low_value
    low_pair = conv_back(
        jnp.concatenate([grad_b, grad_c], axis=1), zp, sig_p, pair_pre, pbuf, dpbuf,
        cp_ref, gcp_ref, gcpb_ref,
    ).astype(BF16)
    lowp_ref[...] = low_pair
    grad_ref[...] = (
        dot(low_gate, wg_ref[...], NT)
        + dot(low_value, wv_ref[...], NT)
        + dot(low_pair, wp_ref[...], NT)
        + dot(low_step, ws_ref[...], NT)
    )


def params():
    return pltpu.CompilerParams(
        dimension_semantics=("arbitrary",), vmem_limit_bytes=60 * 1024 * 1024
    )


def forward_call(lens, tokens, cotangent, whole, sizes):
    rows, width, group, channels, heads, pair = sizes
    blocks = rows // group
    n = pair // 2
    rowed = lambda w: pl.BlockSpec((group, w), lambda i: (i, 0))
    fixed = lambda a: pl.BlockSpec(a.shape, lambda i: (0,) * a.ndim)
    shape = jax.ShapeDtypeStruct
    return pl.pallas_call(
        forward_kernel,
        grid=(blocks,),
        in_specs=[
            pl.BlockSpec(memory_space=pltpu.SMEM),
            rowed(width),
            rowed(width),
            *[fixed(a) for a in whole],
        ],
        out_specs=[
            rowed(width), rowed(channels), rowed(channels), rowed(pair), rowed(heads),
            rowed(channels), rowed(channels),
            pl.BlockSpec((1, n, channels), lambda i: (i, 0, 0)),
            rowed(width),
            pl.BlockSpec((2, group), lambda i: (0, i)),
        ],
        out_shape=[
            shape((rows, width), BF16),
            shape((rows, channels), F32),
            shape((rows, channels), F32),
            shape((rows, pair), F32),
            shape((rows, heads), F32),
            shape((rows, channels), F32),
            shape((rows, channels), F32),
            shape((blocks, n, channels), F32),
            shape((rows, width), F32),
            shape((2, rows), F32),
        ],
        scratch_shapes=[
            pltpu.VMEM((group + 8, channels), F32),
            pltpu.VMEM((group + 8, pair), F32),
            pltpu.VMEM((n, channels), F32),
        ],
        compiler_params=params(),
        name="fwd",
    )(lens, tokens, cotangent, *whole)


def backward_call(lens, stats, saved, weights, small, sizes, full_channels):
    rows, width, group, channels, heads, pair = sizes
    blocks = rows // group
    n = pair // 2
    per = group // 8
    gate_pre, value_pre, pair_pre, step_pre, ssd, ggo, states = saved
    back = lambda w: pl.BlockSpec((group, w), lambda i: (blocks - 1 - i, 0))
    above = lambda w: pl.BlockSpec(
        (8, w), lambda i: (jnp.maximum((blocks - 1 - i) * per - 1, 0), 0)
    )
    fixed = lambda a: pl.BlockSpec(a.shape, lambda i: (0,) * a.ndim)
    total = lambda r, w: pl.BlockSpec((r, w), lambda i: (0, 0))
    shape = jax.ShapeDtypeStruct
    taps = small[0].shape[0]
    sums = [
        (1, channels), (taps, channels), (1, channels), (taps, pair), (1, pair),
        (1, heads), (1, heads), (1, channels),
    ]
    return pl.pallas_call(
        partial(backward_kernel, channels=full_channels),
        grid=(blocks,),
        in_specs=[
            pl.BlockSpec(memory_space=pltpu.SMEM),
            pl.BlockSpec((2, group), lambda i: (0, blocks - 1 - i)),
            back(channels), back(channels), above(channels), back(pair), above(pair),
            back(heads), back(channels), back(channels),
            pl.BlockSpec((1, n, channels), lambda i: (blocks - 1 - i, 0, 0)),
            *[fixed(a) for a in weights],
            *[fixed(a) for a in small],
        ],
        out_specs=[
            back(channels), back(channels), back(channels), back(pair), back(heads),
            back(width), back(1),
            *[total(*s) for s in sums],
        ],
        out_shape=[
            shape((rows, channels), BF16),
            shape((rows, channels), BF16),
            shape((rows, channels), BF16),
            shape((rows, pair), BF16),
            shape((rows, heads), BF16),
            shape((rows, width), F32),
            shape((rows, 1), F32),
            *[shape(s, F32) for s in sums],
        ],
        scratch_shapes=[
            pltpu.VMEM((group + 8, channels), F32),
            pltpu.VMEM((group + 8, pair), F32),
            pltpu.VMEM((group + 8, channels), F32),
            pltpu.VMEM((group + 8, pair), F32),
            pltpu.VMEM((n, channels), F32),
            pltpu.VMEM((1, heads), F32),
        ],
        compiler_params=params(),
        name="bwd",
    )(
        lens, stats, gate_pre, value_pre, value_pre, pair_pre, pair_pre, step_pre, ssd,
        ggo, states, *weights, *small,
    )


def per_device(
    tokens, cotangent, seq_lengths, norm_gain, proj_gate, proj_value, proj_pair,
    proj_step, conv_value, conv_value_bias, conv_pair, conv_pair_bias, step_bias,
    log_rate, skip_gain, gate_gain, proj_out,
):
    rows, width = tokens.shape
    channels, heads, pair = proj_gate.shape[1], proj_step.shape[1], proj_pair.shape[1]
    ways = lax.axis_size("tensor")
    full_channels = channels * ways
    group = min(256, rows)
    sizes = (rows, width, group, channels, heads, pair)
    line = lambda a: a[None, :]
    small = (
        conv_value, line(conv_value_bias), conv_pair, line(conv_pair_bias),
        line(step_bias), line(log_rate), line(skip_gain), line(gate_gain),
    )
    weights = (proj_gate, proj_value, proj_pair, proj_step)
    normed, gate_pre, value_pre, pair_pre, step_pre, ssd, ggo, states, mixed, stats = (
        forward_call(
            seq_lengths, tokens, cotangent,
            (line(norm_gain), *weights, *small, proj_out), sizes,
        )
    )
    stats = lax.psum(stats, "tensor")
    mixed_rows = lax.psum_scatter(mixed, "tensor", scatter_dimension=0, tiled=True)
    (
        gate_out, low_gate, low_value, low_pair, low_step, grad_local, scale,
        g_gain, g_cv, g_cvb, g_cp, g_cpb, g_sb, g_lr, g_sg,
    ) = backward_call(
        seq_lengths, stats, (gate_pre, value_pre, pair_pre, step_pre, ssd, ggo, states),
        weights, small, sizes, full_channels,
    )

    share = rows // ways
    first = lax.axis_index("tensor") * share
    own = lambda a: lax.dynamic_slice_in_dim(a, first, share, 0)
    grad_normed = lax.psum_scatter(grad_local, "tensor", scatter_dimension=0, tiled=True)
    own_tok = own(tokens).astype(F32)
    scale_in = lax.rsqrt(jnp.mean(own_tok * own_tok, axis=1, keepdims=True) + EPS)
    g_norm = jnp.sum(grad_normed * own_tok * scale_in, axis=0)
    scaled_grad = grad_normed * norm_gain[None, :]
    row_dot = jnp.sum(scaled_grad * own_tok, axis=1, keepdims=True)
    grad_wide = scaled_grad * scale_in - own_tok * (scale_in**3 / width) * row_dot
    grad_wide = lax.all_gather(grad_wide, "tensor", axis=0, tiled=True)
    grad_tokens = (cotangent.astype(F32) + grad_wide).astype(BF16)

    live = jnp.arange(rows, dtype=jnp.int32) < jnp.sum(seq_lengths)
    block_out = (
        own_tok + jnp.where(own(live)[:, None], mixed_rows * own(scale), 0.0)
    ).astype(BF16)

    cot_live = jnp.where(live[:, None], cotangent, jnp.zeros_like(cotangent))
    tn = lambda a, b: lax.dot_general(a, b, TN, preferred_element_type=F32)
    g_out = tn(gate_out, cot_live)
    g_gate = tn(normed, low_gate)
    g_value = tn(normed, low_value)
    g_pair = tn(normed, low_pair)
    g_step = tn(normed, low_step)
    g_skip = jnp.sum(g_sg.reshape(heads, HEAD), axis=1)
    g_out, g_gate, g_value = lax.psum((g_out, g_gate, g_value), "dp")
    g_step, g_cv, g_cvb, g_sb, g_lr, g_skip, g_gain = lax.psum(
        (g_step, g_cv, g_cvb[0], g_sb[0], g_lr[0], g_skip, g_gain[0]), "dp"
    )
    g_pair, g_cp, g_cpb, g_norm = lax.psum((g_pair, g_cp, g_cpb[0], g_norm), ("dp", "tensor"))
    return (
        block_out, grad_tokens, g_norm, g_gate, g_value, g_pair, g_step, g_cv, g_cvb,
        g_cp, g_cpb, g_sb, g_lr, g_skip, g_gain, g_out,
    )


def solution(mesh):
    return jax.shard_map(
        per_device,
        mesh=mesh,
        in_specs=(
            P("dp", None),
            P("dp", None),
            P("dp", None),
            P(),
            P(None, "tensor"),
            P(None, "tensor"),
            P(),
            P(None, "tensor"),
            P(None, "tensor"),
            P("tensor"),
            P(),
            P(),
            P("tensor"),
            P("tensor"),
            P("tensor"),
            P("tensor"),
            P("tensor", None),
        ),
        out_specs=(
            P(("dp", "tensor"), None),
            P("dp", None),
            P(),
            P(None, "tensor"),
            P(None, "tensor"),
            P(),
            P(None, "tensor"),
            P(None, "tensor"),
            P("tensor"),
            P(),
            P(),
            P("tensor"),
            P("tensor"),
            P("tensor"),
            P("tensor"),
            P("tensor", None),
        ),
        check_vma=False,
    )
```
